32 devices in a mesh: groups: 2 (over y), seq: 4 (over z), head: 2 (over x), sub: 2 (over core).
Axes of the slice: x: 2, y: 2, z: 4, core: 2. Of those that a mesh axis runs over, the one named last changes fastest.
Arguments:
- query_rows: bfloat16 [32, 128, 8192], P('head', 'sub', ('groups', 'seq')), parts along dimension 2, may hold values from -6 to 6
- key_rows: bfloat16 [32, 128, 8192], P('head', 'sub', ('groups', 'seq')), parts along dimension 2, may hold values from -0.5 to 0.5
- value_rows: bfloat16 [32, 64, 8192], P('head', None, ('groups', 'seq')), parts along dimension 2, may hold values from -6 to 6
- level_weights: bfloat16 [32, 7, 8192], P('head', None, ('groups', 'seq')), parts along dimension 2, may hold values from 0.29882812 to 3
Outputs:
- mixed_output: bfloat16 [32, 64, 8192], P('head', 'sub', ('groups', 'seq')), parts along dimension 2
The draws below stay inside these ranges and needn't reach their ends.
There are 2 independent parts, one for each index of `groups`. The reference program is written for one: setup_inputs(seed, part) draws one part's arguments, and reference() takes and returns one part's arrays. A program takes and returns all parts, laid end to end along the dimension named above; each array names one. Nothing has to cross between parts.
All inputs are finite; a program needn't handle non-finite values.
Results may differ from the reference program's by a relative error of at most 0.0049.
Values sent between devices are 32-bit elements; how exact they have to be, the bound alone decides.
No kernel may reach another device: no remote copies, remote signals or barrier semaphores. Data moves between devices by JAX's collectives and lax.ppermute only.
A program may use at most 128 MiB of HBM per device.

```python
import math
import jax
import jax.numpy as jnp
from jax import lax

H = 32
N = 128
P_SIZE = 64
C = 64
KH = 64
TOKENS = 4096
STRETCHES = 64
LOCAL_BITS = 4
SEQ_BITS = 2
LEVELS = 7
N_SUB = 2


def steps_of(stream_key, shape, split, smallest, high):
    loudness, own = 1.0, jax.random.fold_in(stream_key, 6)
    for axis_at, parts in split:
        draws = jnp.exp(jax.random.uniform(jax.random.fold_in(own, axis_at), (parts,), jnp.float32, smallest / len(split), high / len(split)))
        loudness = loudness * jnp.repeat(draws, shape[axis_at] // parts).reshape([-1 if axis == axis_at else 1 for axis in range(len(shape))])
    return loudness


def noise(own_key, shape, width, most, cuts=(), held_as=jnp.bfloat16):
    drawn = jax.random.normal(own_key, shape, jnp.float32) * width
    if len(cuts) > 0:
        drawn = steps_of(own_key, shape, cuts, -0.22, 0.18) * drawn
    return jnp.clip(drawn, min=-most, max=most).astype(held_as)


def setup_inputs(seed: int = 0, part: int = 0) -> dict:
    keys = jax.random.split(jax.random.key(seed), 5)
    part_keys = jax.random.split(jax.random.fold_in(keys[4], part), 5)
    query_rows = noise(part_keys[0], (H, N, TOKENS), 1.0, 6.0, ((0, 2), (1, 2), (2, 4)))
    key_rows = noise(part_keys[1], (H, N, TOKENS), N ** -0.5, 0.5, ((0, 2), (1, 2), (2, 4)))
    value_rows = noise(part_keys[2], (H, P_SIZE, TOKENS), 1.0, 6.0, ((0, 2), (2, 4)))
    level_weights = jnp.clip(jnp.exp(math.log(3.0) - 2.306499 * jax.random.uniform(part_keys[3], (H, LEVELS, TOKENS), jnp.float32) ** steps_of(part_keys[3], (H, LEVELS, TOKENS), ((0, 2), (2, 4)), -0.2, 0.2)), 0.29882812, 3.0).astype(jnp.bfloat16)
    return {"query_rows": query_rows, "key_rows": key_rows, "value_rows": value_rows, "level_weights": level_weights}


def one_head(operands):
    query_cols, key_cols, value_cols, level_part = operands
    query_part = query_cols.T
    key_part = key_cols.T
    value_part = value_cols.T
    query_f = query_part.reshape(STRETCHES, C, N).astype(jnp.float32)
    key_f = key_part.reshape(STRETCHES, C, N).astype(jnp.float32)
    value_f = value_part.reshape(STRETCHES, C, P_SIZE).astype(jnp.float32)
    weight_f = level_part.astype(jnp.float32)
    causal = jnp.tril(jnp.ones((C, C), jnp.float32)) > 0.5
    diag_weight = weight_f[0].reshape(STRETCHES, C, 1) * (C ** -0.5)
    result = jnp.zeros((STRETCHES, C, P_SIZE), jnp.float32)
    for j in range(N_SUB):
        query_block = query_f[:, :, j * KH:(j + 1) * KH]
        key_block = key_f[:, :, j * KH:(j + 1) * KH]
        scores = jnp.einsum('gtn,gsn->gts', query_block, key_block)
        scores = jnp.where(causal, scores * diag_weight, 0.0).astype(jnp.bfloat16)
        scores = lax.optimization_barrier(scores)
        result = result + jnp.einsum('gts,gsp->gtp', scores.astype(jnp.float32), value_f)
    result = result.reshape(TOKENS, P_SIZE)
    stretch_states = jnp.einsum('gsn,gsp->gnp', key_f, value_f)
    for b in range(LOCAL_BITS + SEQ_BITS):
        block_span = 2 ** b
        pairs = STRETCHES // (2 * block_span)
        sibling = stretch_states.reshape(pairs, 2, block_span, N, P_SIZE).sum(axis=2)[:, 0]
        sibling = lax.optimization_barrier(sibling.astype(jnp.bfloat16))
        upper_queries = query_part.reshape(pairs, 2, block_span * C, N)[:, 1].astype(jnp.float32)
        readout = jnp.einsum('gtn,gnp->gtp', upper_queries, sibling.astype(jnp.float32))
        factor = weight_f[b + 1].reshape(pairs, 2, block_span * C)[:, 1] * ((block_span * C) ** -0.5)
        result = result.reshape(pairs, 2, block_span * C, P_SIZE).at[:, 1].add(readout * factor[..., None])
        result = result.reshape(TOKENS, P_SIZE)
    return result.T.astype(jnp.bfloat16)


def reference(query_rows, key_rows, value_rows, level_weights):
    return lax.map(one_head, (query_rows, key_rows, value_rows, level_weights))
```

```python
import jax
import jax.numpy as jnp
from jax import lax
from jax.experimental import pallas as pl
from jax.experimental.pallas import tpu as pltpu
from jax.sharding import PartitionSpec as P

C = 64
BLOCK = 256
HALF = BLOCK // 2
F32 = jnp.float32
BF16 = jnp.bfloat16


def contract(a, b, da, db):
    return lax.dot_general(a, b, (((da,), (db,)), ((), ())), preferred_element_type=F32)


def own_first(v_ref, h, half, a):
    mine = v_ref[h, pl.ds(pl.multiple_of(a * half, half), half), :]
    other = v_ref[h, pl.ds(pl.multiple_of((1 - a) * half, half), half), :]
    return jnp.concatenate([mine, other], axis=0)


def state_kernel(k_ref, v_ref, same_ref, cross_ref):
    a = lax.axis_index("sub")
    heads, width, tokens = k_ref.shape
    half = v_ref.shape[1] // 2
    left = lax.broadcasted_iota(jnp.int32, (2 * half, 2 * width), 1) < width
    for i in range(heads // 2):
        keys = k_ref[2 * i : 2 * i + 2].reshape(2 * width, tokens)
        low = contract(own_first(v_ref, 2 * i, half, a), keys, 1, 1)
        high = contract(own_first(v_ref, 2 * i + 1, half, a), keys, 1, 1)
        both = jnp.where(left, low, high)
        same_ref[i] = both[:half]
        cross_ref[i] = both[half:]


def local_kernel(q_ref, k_ref, v_ref, w_ref, own_ref, send_ref, wide_ref):
    a = lax.axis_index("sub")
    heads, width, tokens = q_ref.shape
    half = v_ref.shape[1] // 2
    blocks = tokens // BLOCK
    row = lax.broadcasted_iota(jnp.int32, (HALF, HALF), 0)
    col = lax.broadcasted_iota(jnp.int32, (HALF, HALF), 1)
    causal = row <= col
    even = lax.broadcasted_iota(jnp.int32, (1, HALF), 1) < C
    for h in range(heads):
        q = q_ref[h]
        k = k_ref[h]
        v = own_first(v_ref, h, half, a)
        wide_ref[h] = q.astype(F32)
        w = w_ref[h].astype(F32)
        w0 = w[0:1] * C**-0.5
        levels = [w[b + 1 : b + 2] * (2**b * C) ** -0.5 for b in range(w.shape[0] - 1)]

        def diagonal(scores, at):
            now = slice(at, at + HALF)
            upper = jnp.where(even, w0[:, now], levels[0][:, now])
            top = scores[:C] * upper
            bottom = scores[C:] * w0[:, now]
            both = jnp.concatenate([top, bottom], axis=0)
            return jnp.where(causal, both, 0.0).astype(BF16)

        states = []
        for i in range(blocks):
            at = i * BLOCK
            q_i, k_i, v_i = (x[:, at : at + BLOCK] for x in (q, k, v))
            top = contract(k_i[:, :HALF], q_i, 0, 0)
            bottom = contract(k_i[:, HALF:], q_i[:, HALF:], 0, 0)
            first = diagonal(top[:, :HALF], at)
            beside = (top[:, HALF:] * levels[1][:, at + HALF : at + BLOCK]).astype(BF16)
            second = diagonal(bottom, at + HALF)
            out_a = contract(v_i[:, :HALF], first, 1, 0)
            out_b = contract(v_i, jnp.concatenate([beside, second], axis=0), 1, 0)
            out = jnp.concatenate([out_a, out_b], axis=1)
            if i < blocks - 1:
                states.append(contract(v_i, k_i, 1, 1))
            r = 0
            while 2**r < blocks:
                if i >> r & 1:
                    start = (i >> r + 1) << r + 1
                    total = states[start]
                    for e in range(start + 1, start + 2**r):
                        total = total + states[e]
                    read = contract(total.astype(BF16), q_i, 1, 0)
                    out = out + read * levels[r + 2][:, at : at + BLOCK]
                r += 1
            own_ref[h, :, at : at + BLOCK] = out[:half]
            send_ref[h, :, at : at + BLOCK] = out[half:]


def readout(state_pairs, q, factors, half, left):
    rows = []
    for same, cross in state_pairs:
        both = [x.astype(BF16) for x in (same, cross)]
        zero = jnp.zeros_like(both[0])
        rows.append(jnp.concatenate([jnp.where(left, x, zero) for x in both], axis=1))
        rows.append(jnp.concatenate([jnp.where(left, zero, x) for x in both], axis=1))
    read = contract(jnp.concatenate(rows, axis=0), q, 1, 0)
    totals = [None, None]
    for m, pair in enumerate(factors):
        for e in range(2):
            part = read[(2 * m + e) * half : (2 * m + e + 1) * half] * pair[e]
            totals[e] = part if totals[e] is None else totals[e] + part
    return totals


def add_levels(first, level_counts, acc_of, state_refs, q_ref, other_of, w_ref, emit):
    heads, width, tokens = q_ref.shape
    half = state_refs[0].shape[1]
    left = lax.broadcasted_iota(jnp.int32, (half, 2 * width), 1) < width
    for i in range(heads // 2):
        pairs = []
        at = 0
        for count in level_counts:
            refs = state_refs[at : at + 2 * count]
            at += 2 * count
            same, cross = refs[0][i], refs[1][i]
            for e in range(1, count):
                same = same + refs[2 * e][i]
                cross = cross + refs[2 * e + 1][i]
            pairs.append((same, cross))
        q = jnp.concatenate(
            [q_ref[2 * i : 2 * i + 2].reshape(2 * width, tokens), other_of(i)], axis=0
        )
        factors = []
        for m in range(len(level_counts)):
            b = first + m
            factors.append(
                [
                    w_ref[2 * i + e][b + 1 : b + 2].astype(F32) * (2**b * C) ** -0.5
                    for e in range(2)
                ]
            )
        totals = readout(pairs, q, factors, half, left)
        for e in range(2):
            emit(2 * i + e, acc_of(2 * i + e) + totals[e])


def middle_kernel(first, own_ref, got_ref, q_ref, wide_ref, w_ref, same_ref, cross_ref, acc_ref, other_ref):
    _, width, tokens = q_ref.shape

    def other_of(i):
        other = wide_ref[2 * i : 2 * i + 2].astype(BF16)
        other_ref[2 * i : 2 * i + 2] = other
        return other.reshape(2 * width, tokens)

    def emit(h, value):
        acc_ref[h] = value

    add_levels(
        first, [1], lambda h: own_ref[h] + got_ref[h], [same_ref, cross_ref], q_ref, other_of, w_ref, emit
    )


def last_kernel(first, level_counts, acc_ref, q_ref, other_ref, w_ref, *rest):
    _, width, tokens = q_ref.shape
    state_refs, out_ref = rest[:-1], rest[-1]

    def emit(h, value):
        out_ref[h] = value.astype(BF16)

    add_levels(
        first,
        level_counts,
        lambda h: acc_ref[h],
        state_refs,
        q_ref,
        lambda i: other_ref[2 * i : 2 * i + 2].reshape(2 * width, tokens),
        w_ref,
        emit,
    )


def by_heads(kernel, heads_each, arrays, shapes, flops, pair_args=()):
    heads = arrays[0].shape[0]
    steps = heads // heads_each

    def spec(shape):
        return pl.BlockSpec((shape[0] // steps,) + tuple(shape[1:]), lambda i: (i, 0, 0))

    nbytes = sum(x.size * x.dtype.itemsize for x in list(arrays) + list(shapes))
    return pl.pallas_call(
        kernel,
        grid=(steps,),
        in_specs=[spec(x.shape) for x in arrays],
        out_specs=[spec(x.shape) for x in shapes],
        out_shape=list(shapes),
        cost_estimate=pl.CostEstimate(flops=flops, bytes_accessed=nbytes, transcendentals=0),
    )(*arrays)


def on_device(query_rows, key_rows, value_rows, level_weights):
    heads, width, tokens = query_rows.shape
    values = value_rows.shape[1]
    half = values // 2
    local_bits = (tokens // C).bit_length() - 1
    seq = lax.axis_size("seq")
    seq_bits = seq.bit_length() - 1
    swap = [(0, 1), (1, 0)]
    shape = jax.ShapeDtypeStruct
    each = min(4, heads)

    state = shape((heads // 2, half, 2 * width), F32)
    same, cross = by_heads(
        state_kernel, each, [key_rows, value_rows], [state, state], 2 * heads * width * values * tokens
    )
    cross = lax.ppermute(cross, "sub", swap)

    received = []
    for m in range(seq_bits):
        span = 2**m
        bases = range(span, seq, 2 * span)
        got = []
        pieces = [same, cross]
        for j in range(span):
            if j == 0:
                got.append([lax.ppermute(x, "seq", [(b - 1, b) for b in bases]) for x in pieces])
            else:
                got.append(
                    [lax.ppermute(x, "seq", [(b + j - 1, b + j) for b in bases]) for x in got[-1]]
                )
        received.append(got)
        if m + 1 < seq_bits:
            same, cross = same + got[-1][0], cross + got[-1][1]

    part = shape((heads, half, tokens), F32)
    own, send, wide = by_heads(
        local_kernel,
        min(2, heads),
        [query_rows, key_rows, value_rows, level_weights],
        [part, part, shape(query_rows.shape, F32)],
        heads * tokens * width * values * 12,
    )
    got_part = lax.ppermute(send, "sub", swap)
    got_wide = lax.ppermute(wide, "sub", swap)

    import functools

    acc, other = by_heads(
        functools.partial(middle_kernel, local_bits),
        each,
        [own, got_part, query_rows, got_wide, level_weights] + received[0][0],
        [part, shape(query_rows.shape, BF16)],
        2 * heads * 2 * width * half * tokens,
    )
    counts = [len(got) for got in received[1:]]
    flat = [x for got in received[1:] for pair in got for x in pair]
    (out,) = by_heads(
        functools.partial(last_kernel, local_bits + 1, counts),
        each,
        [acc, query_rows, other, level_weights] + flat,
        [shape((heads, half, tokens), BF16)],
        2 * heads * 2 * width * half * tokens,
    )
    return out


def solution(mesh):
    placed = (
        P("head", "sub", ("groups", "seq")),
        P("head", "sub", ("groups", "seq")),
        P("head", None, ("groups", "seq")),
        P("head", None, ("groups", "seq")),
    )
    return jax.shard_map(
        on_device,
        mesh=mesh,
        in_specs=placed,
        out_specs=P("head", "sub", ("groups", "seq")),
        check_vma=False,
    )
```

```python
import functools

import jax
import jax.numpy as jnp
from jax import lax
from jax.experimental import pallas as pl
from jax.experimental.pallas import tpu as pltpu
from jax.sharding import PartitionSpec as P


C = 64
BLOCK = 256
PARTS = 4
HALF = BLOCK // 2
F32 = jnp.float32
BF16 = jnp.bfloat16


def contract(a, b, da, db):
    return lax.dot_general(a, b, (((da,), (db,)), ((), ())), preferred_element_type=F32)


def factor(b):
    return (2 ** max(b - 1, 0) * C) ** -0.5


def own_first(v_ref, h, half, a):
    mine = v_ref[h, pl.ds(pl.multiple_of(a * half, half), half), :]
    other = v_ref[h, pl.ds(pl.multiple_of((1 - a) * half, half), half), :]
    return jnp.concatenate([mine, other], axis=0)


def scaled_weights(w_ref, rows_ref, first):
    for j in range(rows_ref.shape[0]):
        rows_ref[j] = w_ref[first + j].astype(F32) * factor(first + j)


def state_kernel(k_ref, v_ref, same_ref, cross_ref):
    a = lax.axis_index("sub")
    heads, width, tokens = k_ref.shape
    half = v_ref.shape[1] // 2
    left = lax.broadcasted_iota(jnp.int32, (half, 2 * width), 1) < width

    def pair(i, _):
        keys = k_ref[pl.ds(2 * i, 2)].reshape(2 * width, tokens)
        values = jnp.concatenate([own_first(v_ref, 2 * i + e, half, a) for e in range(2)], axis=0)
        both = contract(values, keys, 1, 1)
        same_ref[i] = jnp.where(left, both[:half], both[2 * half : 3 * half])
        cross_ref[i] = jnp.where(left, both[half : 2 * half], both[3 * half :])
        return 0

    lax.fori_loop(0, heads // 2, pair, 0, unroll=2)


def local_kernel(start, q_ref, k_ref, v_ref, w_ref, after_ref, own_ref, send_ref, wide_ref, rows_ref):
    a = lax.axis_index("sub")
    _, _, tokens = q_ref.shape
    half = v_ref.shape[1] // 2
    blocks = tokens // BLOCK
    row = lax.broadcasted_iota(jnp.int32, (HALF, HALF), 0)
    col = lax.broadcasted_iota(jnp.int32, (HALF, HALF), 1)
    causal = row <= col
    even = lax.broadcasted_iota(jnp.int32, (1, HALF), 1) < C
    scaled_weights(w_ref, rows_ref, 0)

    def head(g, _):
        h = start + g
        q = q_ref[h]
        k = k_ref[h]
        v = own_first(v_ref, h, half, a)
        wide_ref[g] = q.astype(F32)
        w0, *levels = [rows_ref[j, pl.ds(h, 1), :] for j in range(rows_ref.shape[0])]

        def diagonal(scores, at):
            now = slice(at, at + HALF)
            upper = jnp.where(even, w0[:, now], levels[0][:, now])
            top = scores[:C] * upper
            bottom = scores[C:] * w0[:, now]
            both = jnp.concatenate([top, bottom], axis=0)
            return jnp.where(causal, both, 0.0).astype(BF16)

        states = []
        for i in range(blocks):
            at = i * BLOCK
            q_i, k_i, v_i = (x[:, at : at + BLOCK] for x in (q, k, v))
            top = contract(k_i[:, :HALF], q_i, 0, 0)
            bottom = contract(k_i[:, HALF:], q_i[:, HALF:], 0, 0)
            first = diagonal(top[:, :HALF], at)
            beside = (top[:, HALF:] * levels[1][:, at + HALF : at + BLOCK]).astype(BF16)
            second = diagonal(bottom, at + HALF)
            out_a = contract(v_i[:, :HALF], first, 1, 0)
            out_b = contract(v_i, jnp.concatenate([beside, second], axis=0), 1, 0)
            out = jnp.concatenate([out_a, out_b], axis=1)
            if i < blocks - 1:
                states.append(contract(v_i, k_i, 1, 1))
            r = 0
            while 2**r < blocks:
                if i >> r & 1:
                    begin = (i >> r + 1) << r + 1
                    total = states[begin]
                    for e in range(begin + 1, begin + 2**r):
                        total = total + states[e]
                    read = contract(total.astype(BF16), q_i, 1, 0)
                    out = out + read * levels[r + 2][:, at : at + BLOCK]
                r += 1
            own_ref[g, :, at : at + BLOCK] = out[:half]
            send_ref[g, :, at : at + BLOCK] = out[half:]
        return 0

    lax.fori_loop(0, own_ref.shape[0], head, 0)


def seq_kernel(start, first, counts, own_ref, got_ref, q_ref, wide_ref, w_ref, *rest):
    state_refs, out_ref, rows_ref = rest[:-2], rest[-2], rest[-1]
    _, width, tokens = q_ref.shape
    half = own_ref.shape[1]
    left = lax.broadcasted_iota(jnp.int32, (half, 2 * width), 1) < width
    scaled_weights(w_ref, rows_ref, first)

    def pair(g, _):
        h = start + 2 * g
        i = start // 2 + g
        rows = []
        at = 0
        for count in counts:
            refs = state_refs[at : at + 2 * count]
            at += 2 * count
            both = [sum([r[i] for r in refs[c + 2 :: 2]], refs[c][i]).astype(BF16) for c in range(2)]
            zero = jnp.zeros_like(both[0])
            rows.append(jnp.concatenate([jnp.where(left, x, zero) for x in both], axis=1))
            rows.append(jnp.concatenate([jnp.where(left, zero, x) for x in both], axis=1))
        q = jnp.concatenate(
            [
                q_ref[pl.ds(h, 2)].reshape(2 * width, tokens),
                wide_ref[pl.ds(2 * g, 2)].astype(BF16).reshape(2 * width, tokens),
            ],
            axis=0,
        )
        read = contract(jnp.concatenate(rows, axis=0), q, 1, 0)
        for e in range(2):
            total = own_ref[2 * g + e] + got_ref[2 * g + e]
            for m in range(len(counts)):
                part = read[(2 * m + e) * half : (2 * m + e + 1) * half]
                total = total + part * rows_ref[m, pl.ds(h + e, 1), :]
            out_ref[2 * g + e] = total.astype(BF16)
        return 0

    lax.fori_loop(0, own_ref.shape[0] // 2, pair, 0)


def in_vmem(kernel, arrays, shapes, scratch, flops):
    whole = pl.BlockSpec(memory_space=pltpu.VMEM)
    nbytes = sum(x.size * x.dtype.itemsize for x in list(arrays) + list(shapes))
    return pl.pallas_call(
        kernel,
        in_specs=[whole] * len(arrays),
        out_specs=[whole] * len(shapes),
        out_shape=list(shapes),
        scratch_shapes=scratch,
        compiler_params=pltpu.CompilerParams(vmem_limit_bytes=4 << 20),
        cost_estimate=pl.CostEstimate(flops=flops, bytes_accessed=nbytes, transcendentals=0),
    )(*arrays)


def on_device(query_rows, key_rows, value_rows, level_weights):
    heads, width, tokens = query_rows.shape
    values = value_rows.shape[1]
    half = values // 2
    local_bits = (tokens // C).bit_length() - 1
    seq = lax.axis_size("seq")
    seq_bits = seq.bit_length() - 1
    swap = [(0, 1), (1, 0)]
    shape = jax.ShapeDtypeStruct
    weights = jnp.transpose(level_weights, (1, 0, 2))

    state = shape((heads // 2, half, 2 * width), F32)
    same, cross = in_vmem(
        state_kernel, [key_rows, value_rows], [state, state], [], 2 * heads * width * values * tokens
    )
    got_cross = lax.ppermute(cross, "sub", swap)

    pieces = [same, got_cross]
    received = []
    for m in range(seq_bits):
        span = 2**m
        bases = range(span, seq, 2 * span)
        got = []
        for j in range(span):
            sources = pieces if j == 0 else got[-1]
            hops = [(b + j - 1, b + j) for b in bases]
            moved = []
            for x in sources:
                moved.append(lax.ppermute(x, "seq", hops))
            got.append(moved)
        received.append(got)
        if m + 1 < seq_bits:
            pieces = [x + y for x, y in zip(pieces, got[-1])]
    counts = [len(got) for got in received]
    flat = [x for got in received for pair in got for x in pair]

    parts = min(PARTS, heads // 2)
    each = heads // parts
    part = shape((each, half, tokens), F32)
    outs = []
    for p in range(parts):
        own, send, wide = in_vmem(
            functools.partial(local_kernel, p * each),
            [query_rows, key_rows, value_rows, weights, cross],
            [part, part, shape((each, width, tokens), F32)],
            [pltpu.VMEM((local_bits + 1, heads, tokens), F32)],
            each * tokens * width * values * 12,
        )
        got_part = lax.ppermute(send, "sub", swap)
        got_wide = lax.ppermute(wide, "sub", swap)
        outs.append((own, got_part, got_wide))
    final = []
    for p, (own, got_part, got_wide) in enumerate(outs):
        (out,) = in_vmem(
            functools.partial(seq_kernel, p * each, local_bits + 1, counts),
            [own, got_part, query_rows, got_wide, weights] + flat,
            [shape((each, half, tokens), BF16)],
            [pltpu.VMEM((seq_bits, heads, tokens), F32)],
            2 * each * 2 * width * half * tokens * seq_bits,
        )
        final.append(out)
    return jnp.concatenate(final, axis=0)


def solution(mesh):
    placed = (
        P("head", "sub", ("groups", "seq")),
        P("head", "sub", ("groups", "seq")),
        P("head", None, ("groups", "seq")),
        P("head", None, ("groups", "seq")),
    )

    return jax.shard_map(
        on_device,
        mesh=mesh,
        in_specs=placed,
        out_specs=P("head", "sub", ("groups", "seq")),
        check_vma=False,
    )
```

```python
import functools

import jax
import jax.numpy as jnp
from jax import lax
from jax.experimental import pallas as pl
from jax.experimental.pallas import tpu as pltpu
from jax.sharding import PartitionSpec as P


C = 64
PAIR = 2 * C
BLOCK = 2 * PAIR
PARTS = 2
F32 = jnp.float32
BF16 = jnp.bfloat16


def contract(a, b, da, db):
    return lax.dot_general(a, b, (((da,), (db,)), ((), ())), preferred_element_type=F32)


def rows(*parts):
    return jnp.concatenate(parts, axis=0)


def lanes(*parts):
    return jnp.concatenate(parts, axis=1)


def factor(level):
    return (2 ** max(level - 1, 0) * C) ** -0.5


def own_first(v_ref, h, half, a):
    mine = v_ref[h, pl.ds(pl.multiple_of(a * half, half), half), :]
    other = v_ref[h, pl.ds(pl.multiple_of((1 - a) * half, half), half), :]
    return rows(mine, other)


def scaled_weights(w_ref, rows_ref, first):
    for j in range(rows_ref.shape[0]):
        rows_ref[j] = w_ref[first + j].astype(F32) * factor(first + j)


def state_kernel(k_hbm, v_hbm, same_ref, cross_ref, k_ref, v_ref, sems):
    a = lax.axis_index("sub")
    heads, width, tokens = k_ref.shape
    half = v_ref.shape[1] // 2
    left = lax.broadcasted_iota(jnp.int32, (half, 2 * width), 1) < width
    chunks = sems.shape[0]
    each = heads // chunks
    copies = []
    for c in range(chunks):
        part = pl.ds(c * each, each)
        copies.append(
            (
                pltpu.make_async_copy(k_hbm.at[part], k_ref.at[part], sems.at[c, 0]),
                pltpu.make_async_copy(v_hbm.at[part], v_ref.at[part], sems.at[c, 1]),
            )
        )
        for copy in copies[-1]:
            copy.start()
    for c in range(chunks):
        for copy in copies[c]:
            copy.wait()
        for i in range(c * each // 2, (c + 1) * each // 2):
            keys = k_ref[2 * i : 2 * i + 2].reshape(2 * width, tokens)
            values = rows(*(own_first(v_ref, 2 * i + e, half, a) for e in range(2)))
            both = contract(values, keys, 1, 1)
            same_ref[i] = jnp.where(left, both[:half], both[2 * half : 3 * half])
            cross_ref[i] = jnp.where(left, both[half : 2 * half], both[3 * half :])


def widen_kernel(q_ref, after_ref, wide_ref):
    def head(h, _):
        wide_ref[h] = q_ref[h].astype(F32)
        return 0

    lax.fori_loop(0, q_ref.shape[0], head, 0, unroll=2)


def local_kernel(start, q_ref, k_ref, v_ref, w_ref, after_ref, own_ref, send_ref, rows_ref):
    a = lax.axis_index("sub")
    _, width, tokens = q_ref.shape
    half = v_ref.shape[1] // 2
    blocks = tokens // BLOCK
    row = lax.broadcasted_iota(jnp.int32, (PAIR, BLOCK), 0)
    col = lax.broadcasted_iota(jnp.int32, (PAIR, BLOCK), 1) % PAIR
    causal = row <= col
    even = lax.broadcasted_iota(jnp.int32, (1, BLOCK), 1) % PAIR < C
    left = lax.broadcasted_iota(jnp.int32, (PAIR, 2 * width), 1) < width
    left_values = lax.broadcasted_iota(jnp.int32, (2 * half, 2 * width), 1) < width
    no_query = jnp.zeros((width, PAIR), BF16)
    no_score = jnp.zeros((PAIR, PAIR), BF16)
    no_key = jnp.zeros((PAIR, 2 * width), BF16)
    scaled_weights(w_ref, rows_ref, 0)

    def head(g, _):
        h = start + g
        q = q_ref[h]
        k = k_ref[h]
        v = own_first(v_ref, h, half, a)
        q_f = q.astype(F32)
        w = [rows_ref[j, pl.ds(h, 1), :] for j in range(rows_ref.shape[0])]
        sums = []
        for i in range(blocks):
            now = slice(i * BLOCK, (i + 1) * BLOCK)
            one = slice(i * BLOCK, i * BLOCK + PAIR)
            two = slice(i * BLOCK + PAIR, (i + 1) * BLOCK)
            k_t = rows(k[:, one], k[:, two]).T
            v_i = v[:, now]
            queries = rows(lanes(q[:, one], no_query), lanes(no_query, q[:, two]))
            scores = contract(k_t, queries, 1, 0)
            upper = jnp.where(even, w[0][:, now], w[1][:, now])
            scores = rows(scores[:C] * upper, scores[C:] * w[0][:, now])
            scores = jnp.where(causal, scores, 0.0).astype(BF16)
            keys = rows(jnp.where(left, k_t, no_key), jnp.where(left, no_key, k_t))
            state = contract(v_i, keys, 1, 0)
            reads = [(state, lanes(no_query, (q_f[:, two] * w[2][:, two]).astype(BF16)))]
            r = 0
            while 2**r < blocks:
                if i >> r & 1:
                    begin = (i >> r + 1) << r + 1
                    total = sums[begin]
                    for e in range(begin + 1, begin + 2**r):
                        total = total + sums[e]
                    reads.append((total, (q_f[:, now] * w[3 + r][:, now]).astype(BF16)))
                r += 1
            if i < blocks - 1:
                sums.append(state + pltpu.roll(state, width, 1))
            lhs = [v_i]
            rhs = [rows(lanes(scores[:, :PAIR], no_score), lanes(no_score, scores[:, PAIR:]))]
            for x in range(0, len(reads) - 1, 2):
                lhs.append(jnp.where(left_values, reads[x][0], reads[x + 1][0]).astype(BF16))
                rhs += [reads[x][1], reads[x + 1][1]]
            if len(reads) % 2:
                lhs.append(reads[-1][0][:, :width].astype(BF16))
                rhs.append(reads[-1][1])
            out = contract(lanes(*lhs), rows(*rhs), 1, 0)
            own_ref[g, :, now] = out[:half]
            send_ref[g, :, now] = out[half:]
        return 0

    lax.fori_loop(0, own_ref.shape[0], head, 0, unroll=min(4, own_ref.shape[0]))


def level_sums(i, counts, state_refs, half, width, q, weight_of):
    if not counts:
        return None
    left = lax.broadcasted_iota(jnp.int32, (half, 2 * width), 1) < width
    lhs = []
    at = 0
    for count in counts:
        refs = state_refs[at : at + 2 * count]
        at += 2 * count
        both = [sum([r[i] for r in refs[c + 2 :: 2]], refs[c][i]).astype(BF16) for c in range(2)]
        zero = jnp.zeros_like(both[0])
        lhs.append(lanes(*(jnp.where(left, x, zero) for x in both)))
        lhs.append(lanes(*(jnp.where(left, zero, x) for x in both)))
    read = contract(rows(*lhs), q, 1, 0)
    totals = []
    for e in range(2):
        total = None
        for m in range(len(counts)):
            part = read[(2 * m + e) * half : (2 * m + e + 1) * half] * weight_of(m, 2 * i + e)
            total = part if total is None else total + part
        totals.append(total)
    return totals


def middle_kernel(first, counts, parts, q_ref, wide_ref, w_ref, *rest):
    own_refs, got_refs = rest[:parts], rest[parts : 2 * parts]
    state_refs = rest[2 * parts : 2 * parts + 2 * sum(counts)]
    acc_ref, other_ref, rows_ref = rest[2 * parts + 2 * sum(counts) :]
    heads, width, tokens = q_ref.shape
    half = acc_ref.shape[1]
    each = heads // parts
    if counts:
        scaled_weights(w_ref, rows_ref, first)
    for p in range(parts):

        def pair(g, _, p=p):
            h = p * each + 2 * g
            other = wide_ref[pl.ds(h, 2)].astype(BF16)
            other_ref[pl.ds(h, 2)] = other
            q = rows(q_ref[pl.ds(h, 2)].reshape(2 * width, tokens), other.reshape(2 * width, tokens))
            weight_of = lambda m, e: rows_ref[m, pl.ds(e, 1), :]
            totals = level_sums(p * each // 2 + g, counts, state_refs, half, width, q, weight_of)
            for e in range(2):
                total = own_refs[p][2 * g + e] + got_refs[p][2 * g + e]
                acc_ref[h + e] = total if totals is None else total + totals[e]
            return 0

        lax.fori_loop(0, each // 2, pair, 0, unroll=min(2, each // 2))


def last_kernel(first, counts, acc_ref, q_ref, other_ref, w_ref, *rest):
    state_refs = rest[: 2 * sum(counts)]
    out_hbm, rows_ref, out_ref, sems = rest[2 * sum(counts) :]
    heads, width, tokens = q_ref.shape
    half = acc_ref.shape[1]
    scaled_weights(w_ref, rows_ref, first)
    copies = []
    for i in range(heads // 2):
        q = rows(
            q_ref[2 * i : 2 * i + 2].reshape(2 * width, tokens),
            other_ref[2 * i : 2 * i + 2].reshape(2 * width, tokens),
        )
        weight_of = lambda m, e: rows_ref[m, e : e + 1, :]
        totals = level_sums(i, counts, state_refs, half, width, q, weight_of)
        for e in range(2):
            out_ref[2 * i + e] = (acc_ref[2 * i + e] + totals[e]).astype(BF16)
        part = pl.ds(2 * i, 2)
        copies.append(pltpu.make_async_copy(out_ref.at[part], out_hbm.at[part], sems.at[i]))
        copies[-1].start()
    for copy in copies:
        copy.wait()


VMEM = pl.BlockSpec(memory_space=pltpu.VMEM)
HBM = pl.BlockSpec(memory_space=pltpu.HBM)


def in_vmem(kernel, arrays, shapes, scratch, flops, in_hbm=0, out_hbm=False):
    nbytes = sum(x.size * x.dtype.itemsize for x in list(arrays) + list(shapes))
    return pl.pallas_call(
        kernel,
        in_specs=[HBM] * in_hbm + [VMEM] * (len(arrays) - in_hbm),
        out_specs=[HBM if out_hbm else VMEM] * len(shapes),
        out_shape=list(shapes),
        scratch_shapes=scratch,
        compiler_params=pltpu.CompilerParams(vmem_limit_bytes=6 << 20),
        cost_estimate=pl.CostEstimate(flops=flops, bytes_accessed=nbytes, transcendentals=0),
    )(*arrays)


def on_device(query_rows, key_rows, value_rows, level_weights):
    heads, width, tokens = query_rows.shape
    values = value_rows.shape[1]
    half = values // 2
    local_bits = (tokens // C).bit_length() - 1
    seq = lax.axis_size("seq")
    seq_bits = seq.bit_length() - 1
    swap = [(0, 1), (1, 0)]
    shape = jax.ShapeDtypeStruct
    like = lambda x: shape(x.shape, x.dtype)
    weights = jnp.transpose(level_weights, (1, 0, 2))

    state = shape((heads // 2, half, 2 * width), F32)
    same, cross, keys, vals = in_vmem(
        state_kernel,
        [pltpu.with_memory_space_constraint(x, pltpu.HBM) for x in (key_rows, value_rows)],
        [state, state, like(key_rows), like(value_rows)],
        [pltpu.SemaphoreType.DMA((min(4, heads // 2), 2))],
        2 * heads * width * values * tokens,
        in_hbm=2,
    )
    got_cross = lax.ppermute(cross, "sub", swap)

    pieces = [same, got_cross]
    received = []
    for m in range(seq_bits):
        span = 2**m
        bases = range(span, seq, 2 * span)
        got = []
        for j in range(span):
            moved = []
            for c in range(2):
                relay = c == 0 and j > 0
                hops = [(b + (j if relay else 0) - 1, b + j) for b in bases]
                moved.append(lax.ppermute(got[-1][c] if relay else pieces[c], "seq", hops))
            got.append(moved)
        received.append(got)
        if m + 1 < seq_bits:
            pieces = [x + y for x, y in zip(pieces, got[-1])]

    (wide,) = in_vmem(widen_kernel, [query_rows, cross], [shape(query_rows.shape, F32)], [], 0)
    got_wide = lax.ppermute(wide, "sub", swap)

    parts = min(PARTS, heads // 2)
    each = heads // parts
    part = shape((each, half, tokens), F32)
    owns, gots = [], []
    for p in range(parts):
        own, send = in_vmem(
            functools.partial(local_kernel, p * each),
            [query_rows, keys, vals, weights, cross],
            [part, part],
            [pltpu.VMEM((local_bits + 1, heads, tokens), F32)],
            each * tokens * width * values * 12,
        )
        gots.append(lax.ppermute(send, "sub", swap))
        owns.append(own)

    counts = [len(got) for got in received]
    flat = [[x for pair in got for x in pair] for got in received]
    acc, other = in_vmem(
        functools.partial(middle_kernel, local_bits + 1, counts[:-1], parts),
        [query_rows, got_wide, weights] + owns + gots + sum(flat[:-1], []),
        [shape((heads, half, tokens), F32), like(query_rows)],
        [pltpu.VMEM((max(seq_bits - 1, 1), heads, tokens), F32)],
        2 * heads * 2 * width * half * tokens,
    )
    (out,) = in_vmem(
        functools.partial(last_kernel, local_bits + seq_bits, counts[-1:]),
        [acc, query_rows, other, weights] + flat[-1],
        [shape((heads, half, tokens), BF16)],
        [
            pltpu.VMEM((1, heads, tokens), F32),
            pltpu.VMEM((heads, half, tokens), BF16),
            pltpu.SemaphoreType.DMA((heads // 2,)),
        ],
        2 * heads * 2 * width * half * tokens,
        out_hbm=True,
    )
    return out


def solution(mesh):
    placed = (
        P("head", "sub", ("groups", "seq")),
        P("head", "sub", ("groups", "seq")),
        P("head", None, ("groups", "seq")),
        P("head", None, ("groups", "seq")),
    )

    return jax.shard_map(
        on_device,
        mesh=mesh,
        in_specs=placed,
        out_specs=P("head", "sub", ("groups", "seq")),
        check_vma=False,
    )
```

```python
import functools

import jax
import jax.numpy as jnp
from jax import lax
from jax.experimental import pallas as pl
from jax.experimental.pallas import tpu as pltpu
from jax.sharding import PartitionSpec as P


C = 64
PAIR = 2 * C
BLOCK = 2 * PAIR
PARTS = 4
F32 = jnp.float32
BF16 = jnp.bfloat16


def contract(a, b, da, db):
    return lax.dot_general(a, b, (((da,), (db,)), ((), ())), preferred_element_type=F32)


def rows(*parts):
    return jnp.concatenate(parts, axis=0)


def lanes(*parts):
    return jnp.concatenate(parts, axis=1)


def factor(level):
    return (2 ** max(level - 1, 0) * C) ** -0.5


def own_first(v_ref, h, half, a):
    mine = v_ref[h, pl.ds(pl.multiple_of(a * half, half), half), :]
    other = v_ref[h, pl.ds(pl.multiple_of((1 - a) * half, half), half), :]
    return rows(mine, other)


def scaled_weights(w_ref, rows_ref, first):
    for j in range(rows_ref.shape[0]):
        rows_ref[j] = w_ref[first + j].astype(F32) * factor(first + j)


def state_kernel(k_hbm, v_hbm, same_ref, cross_ref, k_ref, v_ref, sems):
    a = lax.axis_index("sub")
    heads, width, tokens = k_ref.shape
    half = v_ref.shape[1] // 2
    left = lax.broadcasted_iota(jnp.int32, (half, 2 * width), 1) < width
    chunks = sems.shape[0]
    each = heads // chunks
    copies = []
    for c in range(chunks):
        part = pl.ds(c * each, each)
        copies.append(
            (
                pltpu.make_async_copy(k_hbm.at[part], k_ref.at[part], sems.at[c, 0]),
                pltpu.make_async_copy(v_hbm.at[part], v_ref.at[part], sems.at[c, 1]),
            )
        )
        for copy in copies[-1]:
            copy.start()
    for c in range(chunks):
        for copy in copies[c]:
            copy.wait()
        for i in range(c * each // 2, (c + 1) * each // 2):
            keys = k_ref[2 * i : 2 * i + 2].reshape(2 * width, tokens)
            values = rows(*(own_first(v_ref, 2 * i + e, half, a) for e in range(2)))
            both = contract(values, keys, 1, 1)
            same_ref[i] = jnp.where(left, both[:half], both[2 * half : 3 * half])
            cross_ref[i] = jnp.where(left, both[half : 2 * half], both[3 * half :])


def widen_kernel(q_ref, after_ref, wide_ref):
    def head(h, _):
        wide_ref[h] = q_ref[h].astype(F32)
        return 0

    lax.fori_loop(0, q_ref.shape[0], head, 0, unroll=2)


def local_kernel(start, q_ref, k_ref, v_ref, w_ref, after_ref, own_ref, send_ref, rows_ref):
    a = lax.axis_index("sub")
    _, width, tokens = q_ref.shape
    half = v_ref.shape[1] // 2
    blocks = tokens // BLOCK
    row = lax.broadcasted_iota(jnp.int32, (PAIR, BLOCK), 0)
    col = lax.broadcasted_iota(jnp.int32, (PAIR, BLOCK), 1) % PAIR
    causal = row <= col
    even = lax.broadcasted_iota(jnp.int32, (1, BLOCK), 1) % PAIR < C
    left = lax.broadcasted_iota(jnp.int32, (PAIR, 2 * width), 1) < width
    left_values = lax.broadcasted_iota(jnp.int32, (2 * half, 2 * width), 1) < width
    no_query = jnp.zeros((width, PAIR), BF16)
    no_score = jnp.zeros((PAIR, PAIR), BF16)
    no_key = jnp.zeros((PAIR, 2 * width), BF16)
    scaled_weights(w_ref, rows_ref, 0)

    def head(g, _):
        h = start + g
        q = q_ref[h]
        k = k_ref[h]
        v = own_first(v_ref, h, half, a)
        q_f = q.astype(F32)
        w = [rows_ref[j, pl.ds(h, 1), :] for j in range(rows_ref.shape[0])]
        sums = []
        for i in range(blocks):
            now = slice(i * BLOCK, (i + 1) * BLOCK)
            one = slice(i * BLOCK, i * BLOCK + PAIR)
            two = slice(i * BLOCK + PAIR, (i + 1) * BLOCK)
            k_t = rows(k[:, one], k[:, two]).T
            v_i = v[:, now]
            queries = rows(lanes(q[:, one], no_query), lanes(no_query, q[:, two]))
            scores = contract(k_t, queries, 1, 0)
            upper = jnp.where(even, w[0][:, now], w[1][:, now])
            scores = rows(scores[:C] * upper, scores[C:] * w[0][:, now])
            scores = jnp.where(causal, scores, 0.0).astype(BF16)
            keys = rows(jnp.where(left, k_t, no_key), jnp.where(left, no_key, k_t))
            state = contract(v_i, keys, 1, 0)
            reads = [(state, lanes(no_query, (q_f[:, two] * w[2][:, two]).astype(BF16)))]
            r = 0
            while 2**r < blocks:
                if i >> r & 1:
                    begin = (i >> r + 1) << r + 1
                    total = sums[begin]
                    for e in range(begin + 1, begin + 2**r):
                        total = total + sums[e]
                    reads.append((total, (q_f[:, now] * w[3 + r][:, now]).astype(BF16)))
                r += 1
            if i < blocks - 1:
                sums.append(state + pltpu.roll(state, width, 1))
            lhs = [v_i]
            rhs = [rows(lanes(scores[:, :PAIR], no_score), lanes(no_score, scores[:, PAIR:]))]
            for x in range(0, len(reads) - 1, 2):
                lhs.append(jnp.where(left_values, reads[x][0], reads[x + 1][0]).astype(BF16))
                rhs += [reads[x][1], reads[x + 1][1]]
            if len(reads) % 2:
                lhs.append(reads[-1][0][:, :width].astype(BF16))
                rhs.append(reads[-1][1])
            out = contract(lanes(*lhs), rows(*rhs), 1, 0)
            own_ref[g, :, now] = out[:half]
            send_ref[g, :, now] = out[half:]
        return 0

    lax.fori_loop(0, own_ref.shape[0], head, 0, unroll=min(4, own_ref.shape[0]))


def level_sums(i, counts, state_refs, half, width, q, weight_of):
    if not counts:
        return None
    position = lax.axis_index("seq")
    left = lax.broadcasted_iota(jnp.int32, (half, 2 * width), 1) < width
    lhs = []
    at = 0
    for count in counts:
        refs = state_refs[at : at + 2 * count]
        at += 2 * count
        zero = jnp.zeros((half, 2 * width), BF16)
        both = []
        for c in range(2):
            picked = refs[c][i]
            for j in range(1, count):
                picked = jnp.where(position % count == j, refs[2 * j + c][i], picked)
            both.append(jnp.where((position & count) > 0, picked.astype(BF16), zero))
        lhs.append(lanes(*(jnp.where(left, x, zero) for x in both)))
        lhs.append(lanes(*(jnp.where(left, zero, x) for x in both)))
    read = contract(rows(*lhs), q, 1, 0)
    totals = []
    for e in range(2):
        total = None
        for m in range(len(counts)):
            part = read[(2 * m + e) * half : (2 * m + e + 1) * half] * weight_of(m, 2 * i + e)
            total = part if total is None else total + part
        totals.append(total)
    return totals


def middle_kernel(first, counts, parts, q_ref, wide_ref, w_ref, *rest):
    own_refs, got_refs = rest[:parts], rest[parts : 2 * parts]
    state_refs = rest[2 * parts : 2 * parts + 2 * sum(counts)]
    acc_ref, other_ref, rows_ref = rest[2 * parts + 2 * sum(counts) :]
    heads, width, tokens = q_ref.shape
    half = acc_ref.shape[1]
    each = heads // parts
    if counts:
        scaled_weights(w_ref, rows_ref, first)
    for p in range(parts):

        def pair(g, _, p=p):
            h = p * each + 2 * g
            other = wide_ref[pl.ds(h, 2)].astype(BF16)
            other_ref[pl.ds(h, 2)] = other
            q = rows(q_ref[pl.ds(h, 2)].reshape(2 * width, tokens), other.reshape(2 * width, tokens))
            weight_of = lambda m, e: rows_ref[m, pl.ds(e, 1), :]
            totals = level_sums(p * each // 2 + g, counts, state_refs, half, width, q, weight_of)
            for e in range(2):
                total = own_refs[p][2 * g + e] + got_refs[p][2 * g + e]
                acc_ref[h + e] = total if totals is None else total + totals[e]
            return 0

        lax.fori_loop(0, each // 2, pair, 0, unroll=min(2, each // 2))


def last_kernel(first, counts, acc_ref, q_ref, other_ref, w_ref, *rest):
    state_refs = rest[: 2 * sum(counts)]
    out_hbm, rows_ref, out_ref, sems = rest[2 * sum(counts) :]
    heads, width, tokens = q_ref.shape
    half = acc_ref.shape[1]
    scaled_weights(w_ref, rows_ref, first)
    copies = []
    for i in range(heads // 2):
        q = rows(
            q_ref[2 * i : 2 * i + 2].reshape(2 * width, tokens),
            other_ref[2 * i : 2 * i + 2].reshape(2 * width, tokens),
        )
        weight_of = lambda m, e: rows_ref[m, e : e + 1, :]
        totals = level_sums(i, counts, state_refs, half, width, q, weight_of)
        for e in range(2):
            out_ref[2 * i + e] = (acc_ref[2 * i + e] + totals[e]).astype(BF16)
        part = pl.ds(2 * i, 2)
        copies.append(pltpu.make_async_copy(out_ref.at[part], out_hbm.at[part], sems.at[i]))
        copies[-1].start()
    for copy in copies:
        copy.wait()


VMEM = pl.BlockSpec(memory_space=pltpu.VMEM)
HBM = pl.BlockSpec(memory_space=pltpu.HBM)


def in_vmem(kernel, arrays, shapes, scratch, flops, in_hbm=0, out_hbm=False):
    nbytes = sum(x.size * x.dtype.itemsize for x in list(arrays) + list(shapes))
    return pl.pallas_call(
        kernel,
        in_specs=[HBM] * in_hbm + [VMEM] * (len(arrays) - in_hbm),
        out_specs=[HBM if out_hbm else VMEM] * len(shapes),
        out_shape=list(shapes),
        scratch_shapes=scratch,
        compiler_params=pltpu.CompilerParams(vmem_limit_bytes=6 << 20),
        cost_estimate=pl.CostEstimate(flops=flops, bytes_accessed=nbytes, transcendentals=0),
    )(*arrays)


def swaps(seq, span, step):
    partner = list(range(seq))
    for middle in range(span, seq, 2 * span):
        for near, far in (
            (middle + step - 1, middle + step),
            (middle - step, middle - step - 1),
        ):
            partner[near], partner[far] = far, near
    return list(enumerate(partner))


def on_device(query_rows, key_rows, value_rows, level_weights):
    heads, width, tokens = query_rows.shape
    values = value_rows.shape[1]
    half = values // 2
    local_bits = (tokens // C).bit_length() - 1
    seq = lax.axis_size("seq")
    seq_bits = seq.bit_length() - 1
    swap = [(0, 1), (1, 0)]
    shape = jax.ShapeDtypeStruct
    like = lambda x: shape(x.shape, x.dtype)
    weights = jnp.transpose(level_weights, (1, 0, 2))

    state = shape((heads // 2, half, 2 * width), F32)
    same, cross, keys, vals = in_vmem(
        state_kernel,
        [pltpu.with_memory_space_constraint(x, pltpu.HBM) for x in (key_rows, value_rows)],
        [state, state, like(key_rows), like(value_rows)],
        [pltpu.SemaphoreType.DMA((min(4, heads // 2), 2))],
        2 * heads * width * values * tokens,
        in_hbm=2,
    )
    got_cross = lax.ppermute(cross, "sub", swap)

    pieces = [same, got_cross]
    position = lax.axis_index("seq")
    received = []
    for m in range(seq_bits):
        span = 2**m
        got = []
        for j in range(span):
            hops = swaps(seq, span, j)
            moved = []
            for c in range(2):
                moved.append(lax.ppermute(got[-1][c] if j else pieces[c], "seq", hops))
            got.append(moved)
        received.append(got)
        if m + 1 < seq_bits:
            step = jnp.where(position >> m & 1, position % span, span - 1 - position % span)
            for c in range(2):
                sibling = got[0][c]
                for j in range(1, span):
                    sibling = jnp.where(step == j, got[j][c], sibling)
                pieces[c] = pieces[c] + sibling
        pieces = list(pieces)

    (wide,) = in_vmem(widen_kernel, [query_rows, cross], [shape(query_rows.shape, F32)], [], 0)
    got_wide = lax.ppermute(wide, "sub", swap)

    parts = min(PARTS, heads // 2)
    each = heads // parts
    part = shape((each, half, tokens), F32)
    owns, gots = [], []
    for p in range(parts):
        own, send = in_vmem(
            functools.partial(local_kernel, p * each),
            [query_rows, keys, vals, weights, cross],
            [part, part],
            [pltpu.VMEM((local_bits + 1, heads, tokens), F32)],
            each * tokens * width * values * 12,
        )
        gots.append(lax.ppermute(send, "sub", swap))
        owns.append(own)

    counts = [len(got) for got in received]
    flat = [[x for pair in got for x in pair] for got in received]
    acc, other = in_vmem(
        functools.partial(middle_kernel, local_bits + 1, counts[:-1], parts),
        [query_rows, got_wide, weights] + owns + gots + sum(flat[:-1], []),
        [shape((heads, half, tokens), F32), like(query_rows)],
        [pltpu.VMEM((max(seq_bits - 1, 1), heads, tokens), F32)],
        2 * heads * 2 * width * half * tokens,
    )
    (out,) = in_vmem(
        functools.partial(last_kernel, local_bits + seq_bits, counts[-1:]),
        [acc, query_rows, other, weights] + flat[-1],
        [shape((heads, half, tokens), BF16)],
        [
            pltpu.VMEM((1, heads, tokens), F32),
            pltpu.VMEM((heads, half, tokens), BF16),
            pltpu.SemaphoreType.DMA((heads // 2,)),
        ],
        2 * heads * 2 * width * half * tokens,
        out_hbm=True,
    )
    return out


def solution(mesh):
    placed = (
        P("head", "sub", ("groups", "seq")),
        P("head", "sub", ("groups", "seq")),
        P("head", None, ("groups", "seq")),
        P("head", None, ("groups", "seq")),
    )

    return jax.shard_map(
        on_device,
        mesh=mesh,
        in_specs=placed,
        out_specs=P("head", "sub", ("groups", "seq")),
        check_vma=False,
    )
```
